32 devices in a mesh: seq: 8 (over z, y), kvh: 4 (over x, core).
Axes of the slice: x: 2, y: 2, z: 4, core: 2. Of those that a mesh axis runs over, the one named last changes fastest.
Arguments:
- queries: bfloat16 [1024, 8192], P('seq', 'kvh'), may hold values from -100 to 100
- keys: bfloat16 [1024, 1024], P('seq', 'kvh'), may hold values from -4 to 4
- values: bfloat16 [1024, 1024], P('seq', 'kvh'), may hold values from -6 to 6
- segments: int32 [1024], P('seq'), may hold values from 0 to 2, never falling along the last dimension, each value on 1 to 640 neighbouring positions
- basis: bfloat16 [8, 2, 128, 32], P('kvh'), may hold values from -0.5 to 0.5
Outputs:
- attention: bfloat16 [1024, 8192], P('seq', 'kvh')
- latents: bfloat16 [1024, 512], P('seq', 'kvh')
- captured: float32 [8, 2, 32, 32], P('kvh')
- share: float32 [8, 2], P('kvh')
The draws below stay inside these ranges and needn't reach their ends.
Inputs may be any that keep to these rules, and one draw needn't show every extreme that they name: `segments`: document ids never fall along the sequence, and each document has at most 640 tokens.
All inputs are finite; a program needn't handle non-finite values.
Results may differ from the reference program's by a relative error of at most 0.004.
Values may be sent and summed in bfloat16 or wider, within the bound.
A program may use at most 64 MiB of HBM per device.

```python
import math
import jax
import jax.numpy as jnp
import numpy as np
from jax import lax

HD = 128
QH = 64
KVH = 8
RANK = 32
TOKENS = 1024
DOC_SPAN = 640
DOCS = 3


def shared_keys(key):
    normal_part = jax.random.normal(jax.random.fold_in(key, 101), (TOKENS, KVH, HD), jnp.float32)
    column_scale = jnp.exp(jax.random.uniform(jax.random.fold_in(key, 102), (KVH, HD), jnp.float32, jnp.log(0.5), jnp.log(2.0)))
    mixing = jax.random.normal(jax.random.fold_in(key, 103), (KVH, HD, HD), jnp.float32) / jnp.sqrt(float(HD))
    mix_weight = 0.4
    keyed = normal_part * column_scale[None]
    keyed = keyed + mix_weight * jnp.einsum('tgd,gde->tge', keyed, mixing)
    position = jnp.arange(TOKENS, dtype=jnp.float32) / TOKENS
    keyed = keyed * jnp.exp(0.5 * jnp.log(3.0) * position)[:, None, None]
    keyed = jnp.clip(keyed, -4.0, 4.0)
    return keyed


def draw_keys(key, part):
    keyed = shared_keys(key)
    return keyed.reshape(TOKENS, KVH * HD).astype(jnp.bfloat16)


def draw_queries(key, part):
    query_vals = jnp.clip(jax.random.normal(jax.random.fold_in(key, 107), (TOKENS, KVH, QH // KVH, HD), jnp.float32), -4.0, 4.0)
    return query_vals.reshape(TOKENS, QH * HD).astype(jnp.bfloat16)


def levels(own_key, shape, split, low, top_value):
    def one(dim, blocks):
        steps = jax.random.uniform(jax.random.fold_in(jax.random.fold_in(own_key, 6), dim), (blocks,), jnp.float32, low / len(split), top_value / len(split))
        return jnp.repeat(jnp.exp(steps), shape[dim] // blocks).reshape((-1,) + (1,) * (len(shape) - dim - 1))

    level = one(*split[0])
    for cut in split[1:]:
        level = level * one(*cut)
    return level


def profile(count, total, bound, slope):
    portions = [(1 << 20) // math.isqrt(grade ** slope) + 1 for grade in range(2, count + 1)]
    rest, holding = total - bound - (count - 1), [1] * (count - 1)
    while rest > 0:
        candidates = [i for i in range(count - 1) if holding[i] < bound]
        whole, remaining = sum([portions[i] for i in candidates]), rest
        for i in candidates:
            addition = min(bound - holding[i], max(1, remaining * portions[i] // whole), rest)
            holding[i] = holding[i] + addition
            rest = rest - addition
    return np.array([bound] + holding)


def uneven(rng, count, total, most, lean):
    if count == 2:
        one = jax.random.randint(rng, (), max(1, total - most), min(most, total - 1) + 1)
        return jnp.stack([one, total - one])
    tallies = jnp.asarray(profile(count, total, most, lean), jnp.int32)
    couples = (count - 1) // 2
    source_of, receiver = tallies[1:1 + 2 * couples:2], tallies[2:2 + 2 * couples:2]
    margin = jnp.minimum(source_of - 1, most - receiver)
    passed = jax.random.randint(jax.random.fold_in(rng, 1), (couples,), 0, 1 << 20) % (margin + 1)
    tallies = tallies.at[1:1 + 2 * couples:2].set(source_of - passed).at[2:2 + 2 * couples:2].set(receiver + passed)
    return tallies[jax.random.permutation(jax.random.fold_in(rng, 2), count)]


def normal_values(key, shape, spread, bound, split=(), held_as=jnp.bfloat16):
    drawn = jax.random.normal(key, shape, jnp.float32) * spread
    if len(split) > 0:
        drawn = levels(key, shape, split, -0.22, 0.18) * drawn
    return jnp.clip(drawn, min=-bound, max=bound).astype(held_as)


def setup_inputs(seed: int = 0) -> dict:
    splits = jax.random.split(jax.random.key(seed), 6)
    return {
        "queries": draw_queries(jax.random.fold_in(splits[5], 71), 0),
        "keys": draw_keys(jax.random.fold_in(splits[5], 71), 0),
        "values": normal_values(splits[2], (TOKENS, KVH * HD), 1.0, 6.0, ((0, 8), (1, 4))),
        "segments": jnp.searchsorted(jnp.cumsum(uneven(splits[3], DOCS, TOKENS, DOC_SPAN, 1)), jnp.arange(TOKENS), side="right").astype(jnp.int32),
        "basis": normal_values(splits[4], (KVH, 2, HD, RANK), HD ** -0.5, 0.5, ((0, 4),)),
    }


def reference(queries, keys, values, segments, basis):
    per_group = QH // KVH
    q_heads = queries.reshape(TOKENS, KVH, per_group, HD)
    k_heads = keys.reshape(TOKENS, KVH, HD)
    v_heads = values.reshape(TOKENS, KVH, HD)
    q_block = min(512, TOKENS)
    key_span = min(TOKENS, DOC_SPAN + q_block)
    score_scale = float(HD) ** -0.5

    def attend_block(block_number):
        q_start = (block_number * q_block).astype(jnp.int32)
        k_start = jnp.clip(q_start + q_block - key_span, 0, TOKENS - key_span).astype(jnp.int32)
        q_part = lax.dynamic_slice_in_dim(q_heads, q_start, q_block, 0)
        k_part = lax.dynamic_slice_in_dim(k_heads, k_start, key_span, 0)
        v_part = lax.dynamic_slice_in_dim(v_heads, k_start, key_span, 0)
        seg_query = lax.dynamic_slice_in_dim(segments, q_start, q_block, 0)
        seg_keys = lax.dynamic_slice_in_dim(segments, k_start, key_span, 0)
        query_pos = q_start + jnp.arange(q_block, dtype=jnp.int32)
        key_pos = k_start + jnp.arange(key_span, dtype=jnp.int32)
        allowed = (key_pos[None, :] <= query_pos[:, None]) & (seg_keys[None, :] == seg_query[:, None])
        scores = jnp.einsum('tgjd,sgd->gjts', q_part.astype(jnp.float32), k_part.astype(jnp.float32)) * score_scale
        scores = jnp.where(allowed, scores, -1e30)
        row_max = jnp.max(scores, axis=-1, keepdims=True)
        expo = jnp.where(allowed, jnp.exp(scores - row_max), 0.0)
        row_sum = jnp.sum(expo, axis=-1)
        rounded = lax.optimization_barrier(expo.astype(jnp.bfloat16))
        mixed = jnp.einsum('gjts,sgd->tgjd', rounded.astype(jnp.float32), v_part.astype(jnp.float32))
        mixed = mixed / jnp.transpose(row_sum, (2, 0, 1))[..., None]
        return mixed.astype(jnp.bfloat16)

    attention = lax.map(attend_block, jnp.arange(TOKENS // q_block, dtype=jnp.int32)).reshape(TOKENS, QH * HD)
    k_float = k_heads.astype(jnp.float32)
    v_float = v_heads.astype(jnp.float32)
    gram = jnp.stack([jnp.einsum('tgd,tge->gde', k_float, k_float, precision=lax.Precision.HIGHEST),
                      jnp.einsum('tgd,tge->gde', v_float, v_float, precision=lax.Precision.HIGHEST)], axis=1)
    basis_f32 = basis.astype(jnp.float32)
    captured = jnp.einsum('hcdr,hcde,hces->hcrs', basis_f32, gram, basis_f32, precision=lax.Precision.HIGHEST) / TOKENS
    energy = jnp.trace(gram, axis1=2, axis2=3)
    share = KVH * energy / jnp.sum(energy, axis=0, keepdims=True)
    key_lat = jnp.einsum('tgd,gdr->tgr', k_float, basis_f32[:, 0])
    value_lat = jnp.einsum('tgd,gdr->tgr', v_float, basis_f32[:, 1])
    latents = jnp.concatenate([key_lat, value_lat], axis=-1).astype(jnp.bfloat16).reshape(TOKENS, KVH * 2 * RANK)
    return attention, latents, captured, share
```

```python
import functools
import math

import jax
import jax.numpy as jnp
from jax import lax
from jax.experimental import pallas as pl
from jax.experimental.pallas import tpu as pltpu
from jax.sharding import PartitionSpec as P

MESH = pl.DeviceIdType.MESH
NEG = -1e30


def remote(src, dst, send, recv, device):
    return pltpu.make_async_remote_copy(
        src_ref=src, dst_ref=dst, send_sem=send, recv_sem=recv, device_id=device, device_id_type=MESH
    )


def kernel(
    n, kv_n, reach, heads, group, hd, rank,
    q_hbm, k_hbm, v_hbm, seg_hbm, basis_hbm,
    att_hbm, lat_ref, cap_ref, share_ref,
    qbuf, qt, kbuf, vbuf, segbuf, basis, vt, bias, mx, sums, acc, outv, latf, mine, theirs, ebuf,
    in_sem, out_sem, send_sem, recv_sem, bf_send, bf_recv, e_send, e_recv,
):
    me = lax.axis_index("seq")
    kv = lax.axis_index("kvh")
    odd = lax.rem(me, 2)
    rows = kbuf.shape[1]
    rounds = int(math.log2(n))
    scale = float(hd) ** -0.5 * math.log2(math.e)
    wide = 2 * rows
    chunks = group * rows // wide
    parts = 2 * heads

    loads = [
        pltpu.make_async_copy(src, dst, in_sem.at[i])
        for i, (src, dst) in enumerate(
            [
                (k_hbm, kbuf.at[0]),
                (v_hbm, vbuf.at[0]),
                (seg_hbm, segbuf.at[0]),
                (basis_hbm, basis),
                (q_hbm, qbuf),
            ]
        )
    ]
    for load in loads:
        load.start()

    barrier = pltpu.get_barrier_semaphore()

    def greet(condition, **where):
        @pl.when(condition)
        def _():
            pl.semaphore_signal(barrier, inc=1, device_id=where, device_id_type=MESH)

    count = 0
    for step in (-2, -1, 1, 2):
        inside = (me + step >= 0) & (me + step < n)
        greet(inside, seq=me + step)
        count = count + inside.astype(jnp.int32)

    def partner(r):
        bit = lax.rem(me // (1 << r), 2)
        return me + (1 << r) * (1 - 2 * bit)

    for r in range(2, rounds):
        pl.semaphore_signal(barrier, inc=1, device_id={"seq": partner(r)}, device_id_type=MESH)
    for o in range(1, kv_n):
        pl.semaphore_signal(
            barrier, inc=1, device_id={"kvh": lax.rem(kv + o, kv_n)}, device_id_type=MESH
        )
    pl.semaphore_wait(barrier, count + (rounds - 2) + (kv_n - 1))

    bufs = (segbuf, kbuf, vbuf)
    own = (seg_hbm, k_hbm, v_hbm)

    def routes(e):
        out = []
        if e + 2 <= reach:
            out.append((0, 2, me + 2 < n))
        if e + 1 <= reach:
            out.append((1, 1, odd == 0))
        if e >= 2:
            out.append((1, -1, odd == 1))
        if e + 1 == reach:
            out.append((2, 1, (odd == 1) & (me + 1 < n)))
        return out

    def copies(e, which):
        found = []
        for lane, step, ok in routes(e):
            src = own[which] if e == 0 else bufs[which].at[e]
            copy = remote(
                src,
                bufs[which].at[e + step],
                send_sem.at[e, lane, which],
                recv_sem.at[e + step, which],
                {"seq": me + step},
            )
            found.append((ok & (me >= e), copy))
        return found

    def send(e, which):
        for ok, copy in copies(e, which):
            pl.when(ok)(copy.start)

    def receive(d, which):
        copy = remote(
            bufs[which].at[0],
            bufs[which].at[d],
            send_sem.at[0, 0, which],
            recv_sem.at[d, which],
            {"seq": me},
        )
        pl.when(me >= d)(copy.wait_recv)

    def forward(e):
        for which in range(3):
            receive(e, which)
            send(e, which)

    for which in (1, 2, 0):
        send(0, which)

    for load in loads[:4]:
        load.wait()

    blocks = []
    for g in range(heads):
        cols = slice(g * hd, (g + 1) * hd)
        blocks += [kbuf[0, :, cols], vbuf[0, :, cols]]
    for i in range(parts):
        latf[:, i * rank : (i + 1) * rank] = jnp.dot(
            blocks[i], basis[i // 2, i % 2], preferred_element_type=jnp.float32
        )
    lat = latf[...]
    lat_ref[...] = lat.astype(lat_ref.dtype)
    products = lax.dot_general(
        lat,
        lat,
        (((0,), (0,)), ((), ())),
        precision=lax.Precision.HIGHEST,
        preferred_element_type=jnp.float32,
    )
    column = lax.broadcasted_iota(jnp.int32, (rank, parts * rank), 1) // rank
    seen = jnp.zeros((rank, parts * rank), jnp.float32)
    for i in range(parts):
        seen = jnp.where(column == i, products[i * rank : (i + 1) * rank, :], seen)
    mine[0, :rank, :] = seen
    row = lax.broadcasted_iota(jnp.int32, (8, hd), 0)
    squares = jnp.zeros((8, hd), jnp.float32)
    for i in range(parts):
        block = blocks[i].astype(jnp.float32)
        squares = jnp.where(row == i, jnp.sum(block * block, axis=0, keepdims=True), squares)
    mine[0, rank:, :] = squares

    def butterfly(r):
        return remote(mine.at[r], theirs.at[r], bf_send.at[r], bf_recv.at[r], {"seq": partner(r)})

    def spread(o):
        return remote(
            mine.at[rounds, pl.ds(rank, 8)],
            ebuf.at[o],
            e_send.at[o],
            e_recv.at[o],
            {"kvh": lax.rem(kv + o, kv_n)},
        )

    def finish():
        for o in range(1, kv_n):
            spread(o).wait()
        energy = mine[rounds, rank:, :]
        total = energy
        for o in range(1, kv_n):
            total = total + ebuf[o]
        energy = jnp.sum(energy, axis=1, keepdims=True)
        total = jnp.sum(total, axis=1, keepdims=True)
        for c in range(2):
            whole = total[c : c + 1]
            for g in range(1, heads):
                whole = whole + total[2 * g + c : 2 * g + c + 1]
            for g in range(heads):
                i = 2 * g + c
                share_ref[g : g + 1, c : c + 1] = (heads * kv_n) * energy[i : i + 1] / whole
        for i in range(parts):
            cap_ref[i // 2, i % 2] = mine[rounds, :rank, i * rank : (i + 1) * rank] / (rows * n)

    stage = [0]

    def advance():
        r = stage[0]
        stage[0] += 1
        if r < rounds:
            butterfly(r).wait()
            mine[r + 1] = mine[r] + theirs[r]
            if r + 1 < rounds:
                butterfly(r + 1).start()
            else:
                for o in range(1, kv_n):
                    spread(o).start()
        elif r == rounds:
            finish()

    butterfly(0).start()
    loads[4].wait()

    def turn(h, carry):
        at = pl.ds(pl.multiple_of(h * hd, hd), hd)
        to = pl.ds(pl.multiple_of(h * rows, rows), rows)
        qt[:, to] = qbuf[:, at].T
        return carry

    lax.fori_loop(0, heads * group, turn, 0)

    def attend(d):
        def work():
            seg_q = jnp.broadcast_to(segbuf[0].astype(jnp.float32), (rows, rows))
            seg_k = jnp.broadcast_to(segbuf[d].astype(jnp.float32), (rows, rows)).T
            allowed = seg_q == seg_k
            if d == 0:
                allowed = allowed & (
                    lax.broadcasted_iota(jnp.int32, (rows, rows), 0)
                    <= lax.broadcasted_iota(jnp.int32, (rows, rows), 1)
                )
            hidden = jnp.where(allowed, 0.0, NEG)
            bias[:, :rows] = hidden
            bias[:, rows:] = hidden
            for g in range(heads):
                vt[g] = vbuf[d, :, g * hd : (g + 1) * hd].T

            for g in range(heads):

                def one(c, carry, g=g):
                    at = pl.ds(pl.multiple_of(g * group * rows + c * wide, wide), wide)
                    scores = jnp.dot(
                        kbuf[d, :, g * hd : (g + 1) * hd],
                        qt[:, at],
                        preferred_element_type=jnp.float32,
                    )
                    scores = scores + bias[...]
                    top = jnp.max(scores, axis=0, keepdims=True)
                    if d > 0:
                        before = mx[:, at]
                        top = jnp.maximum(top, before)
                    weights = jnp.exp2((scores - top) * scale)
                    added = jnp.sum(weights, axis=0, keepdims=True)
                    mixed = jnp.dot(
                        vt[g], weights.astype(jnp.bfloat16), preferred_element_type=jnp.float32
                    )
                    if d > 0:
                        factor = jnp.exp2((before - top) * scale)
                        added = added + sums[:, at] * factor
                        mixed = mixed + acc[:, at] * factor
                    mx[:, at] = top
                    sums[:, at] = added
                    acc[:, at] = mixed
                    return carry

                lax.fori_loop(0, chunks, one, 0)

        if d == 0:
            work()
        else:

            @pl.when(me >= d)
            def _():
                if d % 2 == 1:
                    for which in range(3):
                        receive(d, which)
                work()

    attend(0)
    for e in range(2, reach + 1, 2):
        forward(e)
        advance()
        if e >= 4:
            attend(e - 3)
        attend(e)
        advance()
    last_even = reach - reach % 2
    if last_even >= 2:
        attend(last_even - 1)
    while stage[0] <= rounds:
        advance()
    if reach > last_even:
        attend(reach)

    def settle(h, carry):
        at = pl.ds(pl.multiple_of(h * rows, rows), rows)
        to = pl.ds(pl.multiple_of(h * hd, hd), hd)
        mixed = acc[:, at] * (1.0 / sums[:, at])
        outv[:, to] = mixed.T.astype(outv.dtype)
        return carry

    lax.fori_loop(0, heads * group, settle, 0)
    store = pltpu.make_async_copy(outv, att_hbm, out_sem)
    store.start()
    for e in range(0, reach + 1, 2):
        for which in range(3):
            for ok, copy in copies(e, which):
                pl.when(ok)(copy.wait_send)
    store.wait()


def body(n, kv_n, queries, keys, values, segments, basis):
    rows = queries.shape[0]
    heads, _, hd, rank = basis.shape
    group = queries.shape[1] // (heads * hd)
    reach = min(n - 1, n // 2 + 1)
    rounds = int(math.log2(n))
    width = heads * hd
    lanes = heads * group * rows
    f32, bf16 = jnp.float32, jnp.bfloat16
    dma = pltpu.SemaphoreType.DMA
    any_space = pl.BlockSpec(memory_space=pl.ANY)
    vmem = pl.BlockSpec(memory_space=pltpu.VMEM)
    return pl.pallas_call(
        functools.partial(kernel, n, kv_n, reach, heads, group, hd, rank),
        out_shape=(
            jax.ShapeDtypeStruct(queries.shape, bf16),
            jax.ShapeDtypeStruct((rows, heads * 2 * rank), bf16),
            jax.ShapeDtypeStruct((heads, 2, rank, rank), f32),
            jax.ShapeDtypeStruct((heads, 2), f32),
        ),
        in_specs=[any_space] * 5,
        out_specs=(any_space, vmem, vmem, vmem),
        scratch_shapes=[
            pltpu.VMEM(queries.shape, bf16),
            pltpu.VMEM((hd, lanes), bf16),
            pltpu.VMEM((reach + 1, rows, width), bf16),
            pltpu.VMEM((reach + 1, rows, width), bf16),
            pltpu.VMEM((reach + 1, 1, rows), jnp.int32),
            pltpu.VMEM(basis.shape, bf16),
            pltpu.VMEM((heads, hd, rows), bf16),
            pltpu.VMEM((rows, 2 * rows), f32),
            pltpu.VMEM((1, lanes), f32),
            pltpu.VMEM((1, lanes), f32),
            pltpu.VMEM((hd, lanes), f32),
            pltpu.VMEM(queries.shape, bf16),
            pltpu.VMEM((rows, 2 * heads * rank), f32),
            pltpu.VMEM((rounds + 1, rank + 8, hd), f32),
            pltpu.VMEM((rounds, rank + 8, hd), f32),
            pltpu.VMEM((kv_n, 8, hd), f32),
            dma((5,)),
            dma,
            dma((reach + 1, 3, 3)),
            dma((reach + 1, 3)),
            dma((rounds,)),
            dma((rounds,)),
            dma((kv_n,)),
            dma((kv_n,)),
        ],
        compiler_params=pltpu.CompilerParams(collective_id=0, has_side_effects=True),
    )(queries, keys, values, segments.reshape(1, rows), basis)


def solution(mesh):
    placed = (
        P("seq", "kvh"),
        P("seq", "kvh"),
        P("seq", "kvh"),
        P("seq"),
        P("kvh", None, None, None),
    )
    return jax.shard_map(
        functools.partial(body, mesh.shape["seq"], mesh.shape["kvh"]),
        mesh=mesh,
        in_specs=placed,
        out_specs=(P("seq", "kvh"), P("seq", "kvh"), P("kvh", None, None, None), P("kvh", None)),
        check_vma=False,
    )
```

```python
import functools
import math

import jax
import jax.numpy as jnp
from jax import lax
from jax.experimental import pallas as pl
from jax.experimental.pallas import tpu as pltpu
from jax.sharding import PartitionSpec as P

MESH = pl.DeviceIdType.MESH
NEG = -1e30
LIMIT = 24 << 20


def remote(src, dst, send, recv, device):
    return pltpu.make_async_remote_copy(
        src_ref=src, dst_ref=dst, send_sem=send, recv_sem=recv, device_id=device, device_id_type=MESH
    )


def kernel(
    n, kv_n, reach, heads, group, hd, rank,
    q_hbm, k_hbm, v_hbm, seg_hbm, basis_hbm,
    att_ref, lat_ref, cap_ref, share_ref,
    qbuf, qt, kbuf, vbuf, segbuf, basis, vt, bias, mx, sums, acc, latf, mine, theirs, ebuf,
    in_sem, send_sem, recv_sem, bf_send, bf_recv, e_send, e_recv,
):
    me = lax.axis_index("seq")
    kv = lax.axis_index("kvh")
    odd = lax.rem(me, 2)
    rows = kbuf.shape[1]
    rounds = int(math.log2(n))
    scale = float(hd) ** -0.5 * math.log2(math.e)
    wide = 2 * rows
    chunks = group * rows // wide
    parts = 2 * heads
    unroll = reach < 8

    loads = [
        pltpu.make_async_copy(src, dst, in_sem.at[i])
        for i, (src, dst) in enumerate(
            [
                (k_hbm, kbuf.at[0]),
                (v_hbm, vbuf.at[0]),
                (seg_hbm, segbuf.at[0]),
                (basis_hbm, basis),
                (q_hbm, qbuf),
            ]
        )
    ]
    for load in loads:
        load.start()

    barrier = pltpu.get_barrier_semaphore()

    def greet(condition, **where):
        @pl.when(condition)
        def _():
            pl.semaphore_signal(barrier, inc=1, device_id=where, device_id_type=MESH)

    count = 0
    for step in (-2, -1, 1, 2):
        inside = (me + step >= 0) & (me + step < n)
        greet(inside, seq=me + step)
        count = count + inside.astype(jnp.int32)

    def partner(r):
        bit = lax.rem(me // (1 << r), 2)
        return me + (1 << r) * (1 - 2 * bit)

    for r in range(2, rounds):
        pl.semaphore_signal(barrier, inc=1, device_id={"seq": partner(r)}, device_id_type=MESH)
    for o in range(1, kv_n):
        pl.semaphore_signal(
            barrier, inc=1, device_id={"kvh": lax.rem(kv + o, kv_n)}, device_id_type=MESH
        )
    loads[4].wait()

    def turn(h, carry):
        at = pl.ds(pl.multiple_of(h * hd, hd), hd)
        to = pl.ds(pl.multiple_of(h * rows, rows), rows)
        qt[:, to] = qbuf[:, at].T
        return carry

    lax.fori_loop(0, heads * group, turn, 0, unroll=unroll)

    pl.semaphore_wait(barrier, count + (rounds - 2) + (kv_n - 1))

    bufs = (segbuf, kbuf, vbuf)
    own = (seg_hbm, k_hbm, v_hbm)

    def routes(e):
        out = []
        if e + 2 <= reach:
            out.append((0, 2, me + 2 < n))
        if e + 1 <= reach:
            out.append((1, 1, odd == 0))
        if e >= 2:
            out.append((1, -1, odd == 1))
        if e + 1 == reach:
            out.append((2, 1, (odd == 1) & (me + 1 < n)))
        return out

    def copies(e, which):
        found = []
        for lane, step, ok in routes(e):
            src = own[which] if e == 0 else bufs[which].at[e]
            copy = remote(
                src,
                bufs[which].at[e + step],
                send_sem.at[e, lane, which],
                recv_sem.at[e + step, which],
                {"seq": me + step},
            )
            found.append((ok & (me >= e), copy))
        return found

    def send(e, which):
        for ok, copy in copies(e, which):
            pl.when(ok)(copy.start)

    def receive(d, which):
        copy = remote(
            bufs[which].at[0],
            bufs[which].at[d],
            send_sem.at[0, 0, which],
            recv_sem.at[d, which],
            {"seq": me},
        )
        pl.when(me >= d)(copy.wait_recv)

    def forward(e):
        for which in range(3):
            receive(e, which)
            send(e, which)

    for which in (1, 2, 0):
        send(0, which)

    for load in loads[:4]:
        load.wait()

    blocks = []
    for g in range(heads):
        cols = slice(g * hd, (g + 1) * hd)
        blocks += [kbuf[0, :, cols], vbuf[0, :, cols]]
    for i in range(parts):
        latf[:, i * rank : (i + 1) * rank] = lax.dot_general(
            blocks[i],
            basis[i // 2, i % 2],
            (((1,), (1,)), ((), ())),
            preferred_element_type=jnp.float32,
        )
    lat = latf[...]
    lat_ref[...] = lat.astype(lat_ref.dtype)
    products = lax.dot_general(
        lat,
        lat,
        (((0,), (0,)), ((), ())),
        precision=lax.Precision.HIGHEST,
        preferred_element_type=jnp.float32,
    )
    column = lax.broadcasted_iota(jnp.int32, (rank, parts * rank), 1) // rank
    seen = jnp.zeros((rank, parts * rank), jnp.float32)
    for i in range(parts):
        seen = jnp.where(column == i, products[i * rank : (i + 1) * rank, :], seen)
    mine[0, :rank, :] = seen
    row = lax.broadcasted_iota(jnp.int32, (8, hd), 0)
    squares = jnp.zeros((8, hd), jnp.float32)
    for i in range(parts):
        block = blocks[i].astype(jnp.float32)
        squares = jnp.where(row == i, jnp.sum(block * block, axis=0, keepdims=True), squares)
    mine[0, rank:, :] = squares

    def butterfly(r):
        return remote(mine.at[r], theirs.at[r], bf_send.at[r], bf_recv.at[r], {"seq": partner(r)})

    def spread(o):
        return remote(
            mine.at[rounds, pl.ds(rank, 8)],
            ebuf.at[o],
            e_send.at[o],
            e_recv.at[o],
            {"kvh": lax.rem(kv + o, kv_n)},
        )

    def finish():
        for o in range(1, kv_n):
            spread(o).wait()
        energy = mine[rounds, rank:, :]
        total = energy
        for o in range(1, kv_n):
            total = total + ebuf[o]
        energy = jnp.sum(energy, axis=1, keepdims=True)
        total = jnp.sum(total, axis=1, keepdims=True)
        for c in range(2):
            whole = total[c : c + 1]
            for g in range(1, heads):
                whole = whole + total[2 * g + c : 2 * g + c + 1]
            for g in range(heads):
                i = 2 * g + c
                share_ref[g : g + 1, c : c + 1] = (heads * kv_n) * energy[i : i + 1] / whole
        for i in range(parts):
            cap_ref[i // 2, i % 2] = mine[rounds, :rank, i * rank : (i + 1) * rank] / (rows * n)

    stage = [0]

    def advance():
        r = stage[0]
        stage[0] += 1
        if r < rounds:
            butterfly(r).wait()
            mine[r + 1] = mine[r] + theirs[r]
            if r + 1 < rounds:
                butterfly(r + 1).start()
            else:
                for o in range(1, kv_n):
                    spread(o).start()
        elif r == rounds:
            finish()

    butterfly(0).start()
    def attend(d):
        def work():
            seg_q = jnp.broadcast_to(segbuf[0].astype(jnp.float32), (rows, rows))
            seg_k = jnp.broadcast_to(segbuf[d].astype(jnp.float32), (rows, rows)).T
            allowed = seg_q == seg_k
            if d == 0:
                allowed = allowed & (
                    lax.broadcasted_iota(jnp.int32, (rows, rows), 0)
                    <= lax.broadcasted_iota(jnp.int32, (rows, rows), 1)
                )
            hidden = jnp.where(allowed, 0.0, NEG)
            bias[:, :rows] = hidden
            bias[:, rows:] = hidden
            for g in range(heads):
                vt[g] = vbuf[d, :, g * hd : (g + 1) * hd].T

            for g in range(heads):

                def one(c, carry, g=g):
                    at = pl.ds(pl.multiple_of(g * group * rows + c * wide, wide), wide)
                    scores = jnp.dot(
                        kbuf[d, :, g * hd : (g + 1) * hd],
                        qt[:, at],
                        preferred_element_type=jnp.float32,
                    )
                    scores = scores + bias[...]
                    top = jnp.max(scores, axis=0, keepdims=True)
                    if d > 0:
                        before = mx[:, at]
                        top = jnp.maximum(top, before)
                    weights = jnp.exp2((scores - top) * scale)
                    added = jnp.sum(weights, axis=0, keepdims=True)
                    mixed = jnp.dot(
                        vt[g], weights.astype(jnp.bfloat16), preferred_element_type=jnp.float32
                    )
                    if d > 0:
                        factor = jnp.exp2((before - top) * scale)
                        added = added + sums[:, at] * factor
                        mixed = mixed + acc[:, at] * factor
                    mx[:, at] = top
                    sums[:, at] = added
                    acc[:, at] = mixed
                    return carry

                lax.fori_loop(0, chunks, one, 0, unroll=unroll)

        if d == 0:
            work()
        else:

            @pl.when(me >= d)
            def _():
                if d % 2 == 1:
                    for which in range(3):
                        receive(d, which)
                work()

    attend(0)
    for e in range(2, reach + 1, 2):
        forward(e)
        advance()
        if e >= 4:
            attend(e - 3)
        attend(e)
        advance()
    last_even = reach - reach % 2
    if last_even >= 2:
        attend(last_even - 1)
    while stage[0] <= rounds:
        advance()
    if reach > last_even:
        attend(reach)

    for g in range(heads):
        at = slice(g * group * rows, (g + 1) * group * rows)
        att_ref[:, at] = (acc[:, at] * (1.0 / sums[:, at])).astype(att_ref.dtype)
    for e in range(0, reach + 1, 2):
        for which in range(3):
            for ok, copy in copies(e, which):
                pl.when(ok)(copy.wait_send)


def place(
    heads, group, hd, mixed_ref, lat_in, cap_in, share_in,
    att_hbm, lat_ref, cap_ref, share_ref, outv, sem,
):
    rows = outv.shape[0]
    stores = []
    for g in range(heads):
        for h in range(g * group, (g + 1) * group):
            outv[:, h * hd : (h + 1) * hd] = mixed_ref[:, h * rows : (h + 1) * rows].T
        cols = pl.ds(g * group * hd, group * hd)
        store = pltpu.make_async_copy(outv.at[:, cols], att_hbm.at[:, cols], sem.at[g])
        store.start()
        stores.append(store)
    lat_ref[...] = lat_in[...]
    cap_ref[...] = cap_in[...]
    share_ref[...] = share_in[...]
    for store in stores:
        store.wait()


def body(n, kv_n, queries, keys, values, segments, basis):
    rows = queries.shape[0]
    heads, _, hd, rank = basis.shape
    group = queries.shape[1] // (heads * hd)
    reach = min(n - 1, n // 2 + 1)
    rounds = int(math.log2(n))
    width = heads * hd
    lanes = heads * group * rows
    f32, bf16 = jnp.float32, jnp.bfloat16
    dma = pltpu.SemaphoreType.DMA
    hbm = pl.BlockSpec(memory_space=pltpu.HBM)
    vmem = pl.BlockSpec(memory_space=pltpu.VMEM)
    mixed, lat, cap, share = pl.pallas_call(
        functools.partial(kernel, n, kv_n, reach, heads, group, hd, rank),
        out_shape=(
            jax.ShapeDtypeStruct((hd, lanes), bf16),
            jax.ShapeDtypeStruct((rows, heads * 2 * rank), bf16),
            jax.ShapeDtypeStruct((heads, 2, rank, rank), f32),
            jax.ShapeDtypeStruct((heads, 2), f32),
        ),
        in_specs=[hbm] * 5,
        out_specs=(vmem, vmem, vmem, vmem),
        scratch_shapes=[
            pltpu.VMEM(queries.shape, bf16),
            pltpu.VMEM((hd, lanes), bf16),
            pltpu.VMEM((reach + 1, rows, width), bf16),
            pltpu.VMEM((reach + 1, rows, width), bf16),
            pltpu.VMEM((reach + 1, 1, rows), jnp.int32),
            pltpu.VMEM((heads, 2, rank, hd), bf16),
            pltpu.VMEM((heads, hd, rows), bf16),
            pltpu.VMEM((rows, 2 * rows), f32),
            pltpu.VMEM((1, lanes), f32),
            pltpu.VMEM((1, lanes), f32),
            pltpu.VMEM((hd, lanes), f32),
            pltpu.VMEM((rows, 2 * heads * rank), f32),
            pltpu.VMEM((rounds + 1, rank + 8, hd), f32),
            pltpu.VMEM((rounds, rank + 8, hd), f32),
            pltpu.VMEM((kv_n, 8, hd), f32),
            dma((5,)),
            dma((reach + 1, 3, 3)),
            dma((reach + 1, 3)),
            dma((rounds,)),
            dma((rounds,)),
            dma((kv_n,)),
            dma((kv_n,)),
        ],
        compiler_params=pltpu.CompilerParams(
            collective_id=0, has_side_effects=True, vmem_limit_bytes=LIMIT
        ),
    )(queries, keys, values, segments.reshape(1, rows), jnp.swapaxes(basis, 2, 3))
    return pl.pallas_call(
        functools.partial(place, heads, group, hd),
        out_shape=(
            jax.ShapeDtypeStruct(queries.shape, bf16),
            jax.ShapeDtypeStruct(lat.shape, lat.dtype),
            jax.ShapeDtypeStruct(cap.shape, cap.dtype),
            jax.ShapeDtypeStruct(share.shape, share.dtype),
        ),
        in_specs=[vmem] * 4,
        out_specs=(hbm, vmem, vmem, vmem),
        scratch_shapes=[pltpu.VMEM(queries.shape, bf16), dma((heads,))],
        compiler_params=pltpu.CompilerParams(vmem_limit_bytes=LIMIT),
    )(mixed, lat, cap, share)


def solution(mesh):
    placed = (
        P("seq", "kvh"),
        P("seq", "kvh"),
        P("seq", "kvh"),
        P("seq"),
        P("kvh", None, None, None),
    )
    return jax.shard_map(
        functools.partial(body, mesh.shape["seq"], mesh.shape["kvh"]),
        mesh=mesh,
        in_specs=placed,
        out_specs=(P("seq", "kvh"), P("seq", "kvh"), P("kvh", None, None, None), P("kvh", None)),
        check_vma=False,
    )
```

```python
import functools
import math

import jax
import jax.numpy as jnp
from jax import lax
from jax.experimental import pallas as pl
from jax.experimental.pallas import tpu as pltpu
from jax.sharding import PartitionSpec as P

MESH = pl.DeviceIdType.MESH
NEG = -1e30
LIMIT = 24 << 20


def remote(src, dst, send, recv, device):
    return pltpu.make_async_remote_copy(
        src_ref=src, dst_ref=dst, send_sem=send, recv_sem=recv, device_id=device, device_id_type=MESH
    )


def kernel(
    n, kv_n, reach, heads, group, hd, rank,
    q_hbm, k_hbm, v_hbm, seg_hbm, basis_hbm,
    att_ref, lat_ref, cap_ref, share_ref,
    qbuf, qt, kbuf, vbuf, segbuf, basis, vt, bias, mx, sums, acc, latf, mine, theirs, ebuf,
    in_sem, send_sem, recv_sem, bf_send, bf_recv, e_send, e_recv,
):
    me = lax.axis_index("seq")
    kv = lax.axis_index("kvh")
    odd = lax.rem(me, 2)
    rows = kbuf.shape[2]
    rounds = int(math.log2(n))
    scale = float(hd) ** -0.5 * math.log2(math.e)
    wide = 2 * rows
    chunks = group * rows // wide
    parts = 2 * heads
    unroll = reach < 8

    loads = [
        pltpu.make_async_copy(src, dst, in_sem.at[i])
        for i, (src, dst) in enumerate(
            [
                (seg_hbm, segbuf.at[0]),
                (basis_hbm, basis),
                (q_hbm, qbuf),
            ]
            + [
                (src.at[:, pl.ds(g * hd, hd)], dst.at[0, g])
                for g in range(heads)
                for src, dst in ((k_hbm, kbuf), (v_hbm, vbuf))
            ]
        )
    ]
    for load in loads:
        load.start()

    barrier = pltpu.get_barrier_semaphore()

    def greet(condition, **where):
        @pl.when(condition)
        def _():
            pl.semaphore_signal(barrier, inc=1, device_id=where, device_id_type=MESH)

    count = 0
    for step in (-2, -1, 1, 2):
        inside = (me + step >= 0) & (me + step < n)
        greet(inside, seq=me + step)
        count = count + inside.astype(jnp.int32)

    def partner(r):
        bit = lax.rem(me // (1 << r), 2)
        return me + (1 << r) * (1 - 2 * bit)

    for r in range(2, rounds):
        pl.semaphore_signal(barrier, inc=1, device_id={"seq": partner(r)}, device_id_type=MESH)
    for o in range(1, kv_n):
        pl.semaphore_signal(
            barrier, inc=1, device_id={"kvh": lax.rem(kv + o, kv_n)}, device_id_type=MESH
        )

    for load in loads:
        load.wait()

    def turn(h, carry):
        at = pl.ds(pl.multiple_of(h * hd, hd), hd)
        to = pl.ds(pl.multiple_of(h * rows, rows), rows)
        qt[:, to] = qbuf[:, at].T
        return carry

    lax.fori_loop(0, heads * group, turn, 0, unroll=unroll)

    blocks = []
    for g in range(heads):
        blocks += [kbuf[0, g], vbuf[0, g]]
    for i in range(parts):
        latf[:, i * rank : (i + 1) * rank] = lax.dot_general(
            blocks[i],
            basis[i // 2, i % 2],
            (((1,), (1,)), ((), ())),
            preferred_element_type=jnp.float32,
        )
    lat = latf[...]
    lat_ref[...] = lat.astype(lat_ref.dtype)
    products = lax.dot_general(
        lat,
        lat,
        (((0,), (0,)), ((), ())),
        precision=lax.Precision.HIGHEST,
        preferred_element_type=jnp.float32,
    )
    column = lax.broadcasted_iota(jnp.int32, (rank, parts * rank), 1) // rank
    seen = jnp.zeros((rank, parts * rank), jnp.float32)
    for i in range(parts):
        seen = jnp.where(column == i, products[i * rank : (i + 1) * rank, :], seen)
    mine[0, :rank, :] = seen
    row = lax.broadcasted_iota(jnp.int32, (8, hd), 0)
    squares = jnp.zeros((8, hd), jnp.float32)
    for i in range(parts):
        block = blocks[i].astype(jnp.float32)
        squares = jnp.where(row == i, jnp.sum(block * block, axis=0, keepdims=True), squares)
    mine[0, rank:, :] = squares

    pl.semaphore_wait(barrier, count + (rounds - 2) + (kv_n - 1))

    pieces = 1 + parts

    def piece(d, which):
        if which == 0:
            return segbuf.at[d]
        return (kbuf, vbuf)[(which - 1) % 2].at[d, (which - 1) // 2]

    def routes(e):
        out = []
        if e + 2 <= reach:
            out.append((0, 2, me + 2 < n))
        if e + 1 <= reach:
            out.append((1, 1, odd == 0))
        if e >= 2:
            out.append((1, -1, odd == 1))
        if e + 1 == reach:
            out.append((2, 1, (odd == 1) & (me + 1 < n)))
        return out

    def copies(e, which):
        found = []
        for lane, step, ok in routes(e):
            copy = remote(
                piece(e, which),
                piece(e + step, which),
                send_sem.at[e, lane, which],
                recv_sem.at[e + step, which],
                {"seq": me + step},
            )
            found.append((ok & (me >= e), copy))
        return found

    def send(e, which):
        for ok, copy in copies(e, which):
            pl.when(ok)(copy.start)

    def receive(d, which):
        copy = remote(
            piece(0, which),
            piece(d, which),
            send_sem.at[0, 0, which],
            recv_sem.at[d, which],
            {"seq": me},
        )
        pl.when(me >= d)(copy.wait_recv)

    def forward(e):
        for which in range(pieces):
            receive(e, which)
            send(e, which)

    def butterfly(r):
        return remote(mine.at[r], theirs.at[r], bf_send.at[r], bf_recv.at[r], {"seq": partner(r)})

    def spread(o):
        return remote(
            mine.at[rounds, pl.ds(rank, 8)],
            ebuf.at[o],
            e_send.at[o],
            e_recv.at[o],
            {"kvh": lax.rem(kv + o, kv_n)},
        )

    def finish():
        for o in range(1, kv_n):
            spread(o).wait()
        energy = mine[rounds, rank:, :]
        total = energy
        for o in range(1, kv_n):
            total = total + ebuf[o]
        energy = jnp.sum(energy, axis=1, keepdims=True)
        total = jnp.sum(total, axis=1, keepdims=True)
        for c in range(2):
            whole = total[c : c + 1]
            for g in range(1, heads):
                whole = whole + total[2 * g + c : 2 * g + c + 1]
            for g in range(heads):
                i = 2 * g + c
                share_ref[g : g + 1, c : c + 1] = (heads * kv_n) * energy[i : i + 1] / whole
        for i in range(parts):
            cap_ref[i // 2, i % 2] = mine[rounds, :rank, i * rank : (i + 1) * rank] / (rows * n)

    stage = [0]

    def advance():
        r = stage[0]
        stage[0] += 1
        if r < rounds:
            butterfly(r).wait()
            mine[r + 1] = mine[r] + theirs[r]
            if r + 1 < rounds:
                butterfly(r + 1).start()
            else:
                for o in range(1, kv_n):
                    spread(o).start()
        elif r == rounds:
            finish()

    butterfly(0).start()
    for which in range(pieces):
        send(0, which)
    def attend(d):
        def work():
            seg_q = jnp.broadcast_to(segbuf[0].astype(jnp.float32), (rows, rows))
            seg_k = jnp.broadcast_to(segbuf[d].astype(jnp.float32), (rows, rows)).T
            allowed = seg_q == seg_k
            if d == 0:
                allowed = allowed & (
                    lax.broadcasted_iota(jnp.int32, (rows, rows), 0)
                    <= lax.broadcasted_iota(jnp.int32, (rows, rows), 1)
                )
            hidden = jnp.where(allowed, 0.0, NEG)
            bias[:, :rows] = hidden
            bias[:, rows:] = hidden
            for g in range(heads):
                if d % 2 == 1:
                    receive(d, 2 * g + 1)
                    receive(d, 2 * g + 2)
                vt[g] = vbuf[d, g].T

                def one(c, carry, g=g):
                    at = pl.ds(pl.multiple_of(g * group * rows + c * wide, wide), wide)
                    scores = jnp.dot(
                        kbuf[d, g],
                        qt[:, at],
                        preferred_element_type=jnp.float32,
                    )
                    scores = scores + bias[...]
                    top = jnp.max(scores, axis=0, keepdims=True)
                    if d > 0:
                        before = mx[:, at]
                        top = jnp.maximum(top, before)
                    weights = jnp.exp2((scores - top) * scale)
                    added = jnp.sum(weights, axis=0, keepdims=True)
                    mixed = jnp.dot(
                        vt[g], weights.astype(jnp.bfloat16), preferred_element_type=jnp.float32
                    )
                    if d > 0:
                        factor = jnp.exp2((before - top) * scale)
                        added = added + sums[:, at] * factor
                        mixed = mixed + acc[:, at] * factor
                    mx[:, at] = top
                    sums[:, at] = added
                    acc[:, at] = mixed
                    return carry

                lax.fori_loop(0, chunks, one, 0, unroll=unroll)

        if d == 0:
            work()
        else:

            @pl.when(me >= d)
            def _():
                if d % 2 == 1:
                    receive(d, 0)
                work()

    attend(0)
    advance()
    for e in range(2, reach + 1, 2):
        forward(e)
        advance()
        if e >= 4:
            attend(e - 3)
        attend(e)
    last_even = reach - reach % 2
    if last_even >= 2:
        attend(last_even - 1)
    while stage[0] <= rounds:
        advance()
    if reach > last_even:
        attend(reach)

    for g in range(heads):
        at = slice(g * group * rows, (g + 1) * group * rows)
        att_ref[:, at] = (acc[:, at] * (1.0 / sums[:, at])).astype(att_ref.dtype)
    for e in range(0, reach + 1, 2):
        for which in range(pieces):
            for ok, copy in copies(e, which):
                pl.when(ok)(copy.wait_send)


def place(
    heads, group, hd, mixed_ref, lat_in, cap_in, share_in,
    att_hbm, lat_ref, cap_ref, share_ref, outv, sem,
):
    rows = outv.shape[0]
    stores = []
    for g in range(heads):
        for h in range(g * group, (g + 1) * group):
            outv[:, h * hd : (h + 1) * hd] = mixed_ref[:, h * rows : (h + 1) * rows].T
        cols = pl.ds(g * group * hd, group * hd)
        store = pltpu.make_async_copy(outv.at[:, cols], att_hbm.at[:, cols], sem.at[g])
        store.start()
        stores.append(store)
    lat_ref[...] = lat_in[...]
    cap_ref[...] = cap_in[...]
    share_ref[...] = share_in[...]
    for store in stores:
        store.wait()


def body(n, kv_n, queries, keys, values, segments, basis):
    rows = queries.shape[0]
    heads, _, hd, rank = basis.shape
    group = queries.shape[1] // (heads * hd)
    reach = min(n - 1, n // 2 + 1)
    rounds = int(math.log2(n))
    lanes = heads * group * rows
    f32, bf16 = jnp.float32, jnp.bfloat16
    dma = pltpu.SemaphoreType.DMA
    hbm = pl.BlockSpec(memory_space=pltpu.HBM)
    vmem = pl.BlockSpec(memory_space=pltpu.VMEM)
    mixed, lat, cap, share = pl.pallas_call(
        functools.partial(kernel, n, kv_n, reach, heads, group, hd, rank),
        out_shape=(
            jax.ShapeDtypeStruct((hd, lanes), bf16),
            jax.ShapeDtypeStruct((rows, heads * 2 * rank), bf16),
            jax.ShapeDtypeStruct((heads, 2, rank, rank), f32),
            jax.ShapeDtypeStruct((heads, 2), f32),
        ),
        in_specs=[hbm] * 5,
        out_specs=(vmem, vmem, vmem, vmem),
        scratch_shapes=[
            pltpu.VMEM(queries.shape, bf16),
            pltpu.VMEM((hd, lanes), bf16),
            pltpu.VMEM((reach + 1, heads, rows, hd), bf16),
            pltpu.VMEM((reach + 1, heads, rows, hd), bf16),
            pltpu.VMEM((reach + 1, 1, rows), jnp.int32),
            pltpu.VMEM((heads, 2, rank, hd), bf16),
            pltpu.VMEM((heads, hd, rows), bf16),
            pltpu.VMEM((rows, 2 * rows), f32),
            pltpu.VMEM((1, lanes), f32),
            pltpu.VMEM((1, lanes), f32),
            pltpu.VMEM((hd, lanes), f32),
            pltpu.VMEM((rows, 2 * heads * rank), f32),
            pltpu.VMEM((rounds + 1, rank + 8, hd), f32),
            pltpu.VMEM((rounds, rank + 8, hd), f32),
            pltpu.VMEM((kv_n, 8, hd), f32),
            dma((3 + 2 * heads,)),
            dma((reach + 1, 3, 1 + 2 * heads)),
            dma((reach + 1, 1 + 2 * heads)),
            dma((rounds,)),
            dma((rounds,)),
            dma((kv_n,)),
            dma((kv_n,)),
        ],
        compiler_params=pltpu.CompilerParams(
            collective_id=0, has_side_effects=True, vmem_limit_bytes=LIMIT
        ),
    )(*[
        pltpu.with_memory_space_constraint(x, pltpu.HBM)
        for x in (queries, keys, values, segments.reshape(1, rows), jnp.swapaxes(basis, 2, 3))
    ])
    return pl.pallas_call(
        functools.partial(place, heads, group, hd),
        out_shape=(
            jax.ShapeDtypeStruct(queries.shape, bf16),
            jax.ShapeDtypeStruct(lat.shape, lat.dtype),
            jax.ShapeDtypeStruct(cap.shape, cap.dtype),
            jax.ShapeDtypeStruct(share.shape, share.dtype),
        ),
        in_specs=[vmem] * 4,
        out_specs=(hbm, vmem, vmem, vmem),
        scratch_shapes=[pltpu.VMEM(queries.shape, bf16), dma((heads,))],
        compiler_params=pltpu.CompilerParams(vmem_limit_bytes=LIMIT),
    )(mixed, lat, cap, share)


def solution(mesh):
    placed = (
        P("seq", "kvh"),
        P("seq", "kvh"),
        P("seq", "kvh"),
        P("seq"),
        P("kvh", None, None, None),
    )
    return jax.shard_map(
        functools.partial(body, mesh.shape["seq"], mesh.shape["kvh"]),
        mesh=mesh,
        in_specs=placed,
        out_specs=(P("seq", "kvh"), P("seq", "kvh"), P("kvh", None, None, None), P("kvh", None)),
        check_vma=False,
    )
```

```python
import functools
import math

import jax
import jax.numpy as jnp
from jax import lax
from jax.experimental import pallas as pl
from jax.experimental.pallas import tpu as pltpu
from jax.sharding import PartitionSpec as P

MESH = pl.DeviceIdType.MESH
NEG = -1e30
LIMIT = 24 << 20


def remote(src, dst, send, recv, device):
    return pltpu.make_async_remote_copy(
        src_ref=src, dst_ref=dst, send_sem=send, recv_sem=recv, device_id=device, device_id_type=MESH
    )


def kernel(
    n, kv_n, reach, heads, group, hd, rank,
    q_hbm, k_hbm, v_hbm, seg_hbm, basis_hbm,
    att_ref, lat_ref, cap_ref, share_ref,
    qbuf, qt, kbuf, vbuf, segbuf, basis, vt, bias, mx, sums, acc, latf, mine, theirs, ebuf,
    in_sem, send_sem, recv_sem, bf_send, bf_recv, e_send, e_recv,
):
    me = lax.axis_index("seq")
    kv = lax.axis_index("kvh")
    odd = lax.rem(me, 2)
    rows = kbuf.shape[2]
    rounds = int(math.log2(n))
    scale = float(hd) ** -0.5 * math.log2(math.e)
    wide = 2 * rows
    chunks = group * rows // wide
    parts = 2 * heads
    unroll = reach < 8

    loads = [
        pltpu.make_async_copy(src, dst, in_sem.at[i])
        for i, (src, dst) in enumerate(
            [
                (seg_hbm, segbuf.at[0]),
                (basis_hbm, basis),
                (q_hbm, qbuf),
            ]
            + [
                (src.at[:, pl.ds(g * hd, hd)], dst.at[0, g])
                for g in range(heads)
                for src, dst in ((k_hbm, kbuf), (v_hbm, vbuf))
            ]
        )
    ]
    for load in loads:
        load.start()

    barrier = pltpu.get_barrier_semaphore()

    def greet(condition, **where):
        @pl.when(condition)
        def _():
            pl.semaphore_signal(barrier, inc=1, device_id=where, device_id_type=MESH)

    count = 0
    for step in (-2, -1, 1, 2):
        inside = (me + step >= 0) & (me + step < n)
        greet(inside, seq=me + step)
        count = count + inside.astype(jnp.int32)

    def partner(r):
        bit = lax.rem(me // (1 << r), 2)
        return me + (1 << r) * (1 - 2 * bit)

    for r in range(2, rounds):
        pl.semaphore_signal(barrier, inc=1, device_id={"seq": partner(r)}, device_id_type=MESH)
    for o in range(1, kv_n):
        pl.semaphore_signal(
            barrier, inc=1, device_id={"kvh": lax.rem(kv + o, kv_n)}, device_id_type=MESH
        )

    for load in loads:
        load.wait()

    def turn(h, carry):
        at = pl.ds(pl.multiple_of(h * hd, hd), hd)
        to = pl.ds(pl.multiple_of(h * rows, rows), rows)
        qt[:, to] = qbuf[:, at].T
        return carry

    lax.fori_loop(0, heads * group, turn, 0, unroll=unroll)

    blocks = []
    for g in range(heads):
        blocks += [kbuf[0, g], vbuf[0, g]]
    for i in range(parts):
        latf[:, i * rank : (i + 1) * rank] = lax.dot_general(
            blocks[i],
            basis[i // 2, i % 2],
            (((1,), (1,)), ((), ())),
            preferred_element_type=jnp.float32,
        )
    lat = latf[...]
    lat_ref[...] = lat.astype(lat_ref.dtype)
    products = lax.dot_general(
        lat,
        lat,
        (((0,), (0,)), ((), ())),
        precision=lax.Precision.HIGHEST,
        preferred_element_type=jnp.float32,
    )
    column = lax.broadcasted_iota(jnp.int32, (rank, parts * rank), 1) // rank
    seen = jnp.zeros((rank, parts * rank), jnp.float32)
    for i in range(parts):
        seen = jnp.where(column == i, products[i * rank : (i + 1) * rank, :], seen)
    mine[0, :rank, :] = seen
    row = lax.broadcasted_iota(jnp.int32, (8, hd), 0)
    squares = jnp.zeros((8, hd), jnp.float32)
    for i in range(parts):
        block = blocks[i].astype(jnp.float32)
        squares = jnp.where(row == i, jnp.sum(block * block, axis=0, keepdims=True), squares)
    mine[0, rank:, :] = squares

    pl.semaphore_wait(barrier, count + (rounds - 2) + (kv_n - 1))

    pieces = 1 + parts

    def piece(d, which):
        if which == 0:
            return segbuf.at[d]
        return (kbuf, vbuf)[(which - 1) % 2].at[d, (which - 1) // 2]

    def routes(e):
        out = []
        if e + 2 <= reach:
            out.append((0, 2, me + 2 < n))
        if e + 1 <= reach:
            out.append((1, 1, odd == 0))
        if e >= 2:
            out.append((1, -1, odd == 1))
        if e + 1 == reach:
            out.append((2, 1, (odd == 1) & (me + 1 < n)))
        return out

    def copies(e, which):
        found = []
        for lane, step, ok in routes(e):
            copy = remote(
                piece(e, which),
                piece(e + step, which),
                send_sem.at[e, lane, which],
                recv_sem.at[e + step, which],
                {"seq": me + step},
            )
            found.append((ok & (me >= e), copy))
        return found

    def send(e, which):
        for ok, copy in copies(e, which):
            pl.when(ok)(copy.start)

    def receive(d, which):
        copy = remote(
            piece(0, which),
            piece(d, which),
            send_sem.at[0, 0, which],
            recv_sem.at[d, which],
            {"seq": me},
        )
        pl.when(me >= d)(copy.wait_recv)

    def forward(e):
        for which in range(pieces):
            receive(e, which)
            send(e, which)

    def butterfly(r):
        return remote(
            mine.at[r + min(r, 1)], theirs.at[r], bf_send.at[r], bf_recv.at[r], {"seq": partner(r)})

    def spread(o):
        return remote(
            mine.at[1, pl.ds(rank, 8)],
            ebuf.at[o],
            e_send.at[o],
            e_recv.at[o],
            {"kvh": lax.rem(kv + o, kv_n)},
        )

    def gather():
        for o in range(1, kv_n):
            spread(o).wait()
        energy = mine[1, rank:, :]
        total = energy
        for o in range(1, kv_n):
            total = total + ebuf[o]
        for c in range(2):
            whole = total[c : c + 1]
            for g in range(1, heads):
                whole = whole + total[2 * g + c : 2 * g + c + 1]
            energy = jnp.where(row == parts + c, whole, energy)
        mine[2, :rank, :] = mine[1, :rank, :]
        mine[2, rank:, :] = energy

    def finish():
        final = rounds + 1
        energy = jnp.sum(mine[final, rank:, :], axis=1, keepdims=True)
        for i in range(parts):
            c = parts + i % 2
            share_ref[i // 2 : i // 2 + 1, i % 2 : i % 2 + 1] = (
                (heads * kv_n) * energy[i : i + 1] / energy[c : c + 1]
            )
            cap_ref[i // 2, i % 2] = mine[final, :rank, i * rank : (i + 1) * rank] / (rows * n)

    stage = [0]

    def advance():
        r = stage[0]
        stage[0] += 1
        if r == 0:
            butterfly(0).wait()
            mine[1] = mine[0] + theirs[0]
            for o in range(1, kv_n):
                spread(o).start()
        elif r == 1:
            gather()
            butterfly(1).start()
        elif r <= rounds:
            butterfly(r - 1).wait()
            mine[r + 1] = mine[r] + theirs[r - 1]
            if r < rounds:
                butterfly(r).start()
            else:
                finish()

    butterfly(0).start()
    for which in range(pieces):
        send(0, which)
    def attend(d):
        def work():
            seg_q = jnp.broadcast_to(segbuf[0].astype(jnp.float32), (rows, rows))
            seg_k = jnp.broadcast_to(segbuf[d].astype(jnp.float32), (rows, rows)).T
            allowed = seg_q == seg_k
            if d == 0:
                allowed = allowed & (
                    lax.broadcasted_iota(jnp.int32, (rows, rows), 0)
                    <= lax.broadcasted_iota(jnp.int32, (rows, rows), 1)
                )
            hidden = jnp.where(allowed, 0.0, NEG)
            bias[:, :rows] = hidden
            bias[:, rows:] = hidden
            for g in range(heads):
                if d % 2 == 1:
                    receive(d, 2 * g + 1)
                    receive(d, 2 * g + 2)
                vt[g] = vbuf[d, g].T

                def one(c, carry, g=g):
                    at = pl.ds(pl.multiple_of(g * group * rows + c * wide, wide), wide)
                    scores = jnp.dot(
                        kbuf[d, g],
                        qt[:, at],
                        preferred_element_type=jnp.float32,
                    )
                    scores = scores + bias[...]
                    top = jnp.max(scores, axis=0, keepdims=True)
                    if d > 0:
                        before = mx[:, at]
                        top = jnp.maximum(top, before)
                    weights = jnp.exp2((scores - top) * scale)
                    added = jnp.sum(weights, axis=0, keepdims=True)
                    mixed = jnp.dot(
                        vt[g], weights.astype(jnp.bfloat16), preferred_element_type=jnp.float32
                    )
                    if d > 0:
                        factor = jnp.exp2((before - top) * scale)
                        added = added + sums[:, at] * factor
                        mixed = mixed + acc[:, at] * factor
                    mx[:, at] = top
                    sums[:, at] = added
                    acc[:, at] = mixed
                    return carry

                lax.fori_loop(0, chunks, one, 0, unroll=unroll)

        if d == 0:
            work()
        else:

            @pl.when(me >= d)
            def _():
                if d % 2 == 1:
                    receive(d, 0)
                work()

    attend(0)
    advance()
    for e in range(2, reach + 1, 2):
        forward(e)
        advance()
        if e >= 4:
            attend(e - 3)
        attend(e)
    last_even = reach - reach % 2
    if last_even >= 2:
        attend(last_even - 1)
    while stage[0] <= rounds:
        advance()
    if reach > last_even:
        attend(reach)

    for g in range(heads):
        at = slice(g * group * rows, (g + 1) * group * rows)
        att_ref[:, at] = (acc[:, at] * (1.0 / sums[:, at])).astype(att_ref.dtype)
    for e in range(0, reach + 1, 2):
        for which in range(pieces):
            for ok, copy in copies(e, which):
                pl.when(ok)(copy.wait_send)


def place(
    heads, group, hd, mixed_ref, lat_in, cap_in, share_in,
    att_hbm, lat_ref, cap_ref, share_ref, outv, sem,
):
    rows = outv.shape[0]
    stores = []
    for g in range(heads):
        for h in range(g * group, (g + 1) * group):
            outv[:, h * hd : (h + 1) * hd] = mixed_ref[:, h * rows : (h + 1) * rows].T
        cols = pl.ds(g * group * hd, group * hd)
        store = pltpu.make_async_copy(outv.at[:, cols], att_hbm.at[:, cols], sem.at[g])
        store.start()
        stores.append(store)
    lat_ref[...] = lat_in[...]
    cap_ref[...] = cap_in[...]
    share_ref[...] = share_in[...]
    for store in stores:
        store.wait()


def body(n, kv_n, queries, keys, values, segments, basis):
    rows = queries.shape[0]
    heads, _, hd, rank = basis.shape
    group = queries.shape[1] // (heads * hd)
    reach = min(n - 1, n // 2 + 1)
    rounds = int(math.log2(n))
    lanes = heads * group * rows
    f32, bf16 = jnp.float32, jnp.bfloat16
    dma = pltpu.SemaphoreType.DMA
    hbm = pl.BlockSpec(memory_space=pltpu.HBM)
    vmem = pl.BlockSpec(memory_space=pltpu.VMEM)
    mixed, lat, cap, share = pl.pallas_call(
        functools.partial(kernel, n, kv_n, reach, heads, group, hd, rank),
        out_shape=(
            jax.ShapeDtypeStruct((hd, lanes), bf16),
            jax.ShapeDtypeStruct((rows, heads * 2 * rank), bf16),
            jax.ShapeDtypeStruct((heads, 2, rank, rank), f32),
            jax.ShapeDtypeStruct((heads, 2), f32),
        ),
        in_specs=[hbm] * 5,
        out_specs=(vmem, vmem, vmem, vmem),
        scratch_shapes=[
            pltpu.VMEM(queries.shape, bf16),
            pltpu.VMEM((hd, lanes), bf16),
            pltpu.VMEM((reach + 1, heads, rows, hd), bf16),
            pltpu.VMEM((reach + 1, heads, rows, hd), bf16),
            pltpu.VMEM((reach + 1, 1, rows), jnp.int32),
            pltpu.VMEM((heads, 2, rank, hd), bf16),
            pltpu.VMEM((heads, hd, rows), bf16),
            pltpu.VMEM((rows, 2 * rows), f32),
            pltpu.VMEM((1, lanes), f32),
            pltpu.VMEM((1, lanes), f32),
            pltpu.VMEM((hd, lanes), f32),
            pltpu.VMEM((rows, 2 * heads * rank), f32),
            pltpu.VMEM((rounds + 2, rank + 8, hd), f32),
            pltpu.VMEM((rounds, rank + 8, hd), f32),
            pltpu.VMEM((kv_n, 8, hd), f32),
            dma((3 + 2 * heads,)),
            dma((reach + 1, 3, 1 + 2 * heads)),
            dma((reach + 1, 1 + 2 * heads)),
            dma((rounds,)),
            dma((rounds,)),
            dma((kv_n,)),
            dma((kv_n,)),
        ],
        compiler_params=pltpu.CompilerParams(
            collective_id=0, has_side_effects=True, vmem_limit_bytes=LIMIT
        ),
    )(*[
        pltpu.with_memory_space_constraint(x, pltpu.HBM)
        for x in (queries, keys, values, segments.reshape(1, rows), jnp.swapaxes(basis, 2, 3))
    ])
    return pl.pallas_call(
        functools.partial(place, heads, group, hd),
        out_shape=(
            jax.ShapeDtypeStruct(queries.shape, bf16),
            jax.ShapeDtypeStruct(lat.shape, lat.dtype),
            jax.ShapeDtypeStruct(cap.shape, cap.dtype),
            jax.ShapeDtypeStruct(share.shape, share.dtype),
        ),
        in_specs=[vmem] * 4,
        out_specs=(hbm, vmem, vmem, vmem),
        scratch_shapes=[pltpu.VMEM(queries.shape, bf16), dma((heads,))],
        compiler_params=pltpu.CompilerParams(vmem_limit_bytes=LIMIT),
    )(mixed, lat, cap, share)


def solution(mesh):
    placed = (
        P("seq", "kvh"),
        P("seq", "kvh"),
        P("seq", "kvh"),
        P("seq"),
        P("kvh", None, None, None),
    )
    return jax.shard_map(
        functools.partial(body, mesh.shape["seq"], mesh.shape["kvh"]),
        mesh=mesh,
        in_specs=placed,
        out_specs=(P("seq", "kvh"), P("seq", "kvh"), P("kvh", None, None, None), P("kvh", None)),
        check_vma=False,
    )
```
